32 devices in a mesh: section: 4 (over y, core), seq: 8 (over z, x).
Axes of the slice: x: 2, y: 2, z: 4, core: 2. Of those that a mesh axis runs over, the one named last changes fastest.
Arguments:
- pending_residual: bfloat16 [4, 4096, 1536], P('section', 'seq'), may hold values from -32 to 32
- intragroup_mixing_matrix: bfloat16 [4, 8, 512, 512], P('section', 'seq'), may hold values from -0.25 to 0.25
- intergroup_mixing_matrix: bfloat16 [4, 512, 8, 8], P('section', 'seq'), may hold values from -2 to 2
- token_rescale_factor: float32 [4, 1536], P('section'), may hold values from 0.1 to 1.9
- gating_diagonal_matrix: bfloat16 [4, 1536, 768], P('section', 'seq'), may hold values from -0.3125 to 0.3125
- expanding_diagonal_matrix: bfloat16 [4, 1536, 768], P('section', 'seq'), may hold values from -0.3125 to 0.3125
- contracting_diagonal_matrix: bfloat16 [4, 3072, 384], P('section', 'seq'), may hold values from -0.21875 to 0.21875
- feature_rescale_factor: float32 [4, 1536], P('section'), may hold values from 0.1 to 1.9
Outputs:
- advanced: bfloat16 [4, 4096, 1536], P('section', 'seq')
The draws below stay inside these ranges and needn't reach their ends.
All inputs are finite; a program needn't handle non-finite values.
Results may differ from the reference program's by a relative error of at most 0.0051.
Values may be sent and summed in bfloat16 or wider, within the bound.
A program may use at most 64 MiB of HBM per device.

```python
import math
import jax
import jax.numpy as jnp
from jax import lax

D = 1536
FF = 3072
NB = 4
B1 = 512
TOKENS = 4096
B2 = 8
N_SECTION = 4


def draw_pending_residual(key, part):
    first, second, third = jax.random.split(key, 3)
    array_shape = (N_SECTION, TOKENS, D)
    columns = jnp.exp(jax.random.uniform(third, (1, 1, D), jnp.float32, math.log(0.5), math.log(2.0)))
    base = jnp.clip(jax.random.normal(first, array_shape, jnp.float32), -4.0, 4.0)
    rows = jnp.exp(jax.random.uniform(second, (N_SECTION, TOKENS, 1), jnp.float32, math.log(1.0 / 3.0), math.log(3.0)))
    return (base * rows * columns).astype(jnp.bfloat16)


def shard_levels(own_key, extent, cuts, low, high):
    level = 1.0
    for dim, shards_of in cuts:
        heights = jax.random.uniform(jax.random.fold_in(jax.random.fold_in(own_key, 6), dim), (shards_of,), jnp.float32, low / len(cuts), high / len(cuts))
        level = level * jnp.repeat(jnp.exp(heights), extent[dim] // shards_of).reshape((-1,) + (1,) * (len(extent) - 1 - dim))
    return level


def centred(rng, extent, deviation, reach, shards=(), held_as=jnp.bfloat16):
    level = shard_levels(rng, extent, shards, -0.22, 0.18) if shards else 1.0
    entries = jax.random.normal(rng, extent, jnp.float32) * deviation * level
    return jnp.minimum(jnp.maximum(entries, -reach), reach).astype(held_as)


def setup_inputs(seed: int = 0) -> dict:
    key_of = jax.random.split(jax.random.key(seed), 9)
    pending_residual = draw_pending_residual(jax.random.fold_in(key_of[8], 71), 0)
    intragroup_mixing_matrix = centred(key_of[1], (N_SECTION, B2, B1, B1), B1 ** -0.5, 0.25, ((0, 4), (1, 8)))
    intergroup_mixing_matrix = centred(key_of[2], (N_SECTION, B1, B2, B2), B2 ** -0.5, 2.0, ((0, 4), (1, 8)))
    token_rescale_factor = jnp.clip(1.0 + 0.18 * jax.random.normal(key_of[3], (N_SECTION, D), jnp.float32), 0.1, 1.9)
    gating_diagonal_matrix = centred(key_of[4], (N_SECTION, D, FF // NB), (D // NB) ** -0.5, 0.3125, ((0, 4), (1, 8)))
    expanding_diagonal_matrix = centred(key_of[5], (N_SECTION, D, FF // NB), (D // NB) ** -0.5, 0.3125, ((0, 4), (1, 8)))
    contracting_diagonal_matrix = centred(key_of[6], (N_SECTION, FF, D // NB), (FF // NB) ** -0.5, 0.21875, ((0, 4), (1, 8)))
    feature_rescale_factor = jnp.clip(1.0 + 0.18 * jax.random.normal(key_of[7], (N_SECTION, D), jnp.float32), 0.1, 1.9)
    return dict(pending_residual=pending_residual, intragroup_mixing_matrix=intragroup_mixing_matrix, intergroup_mixing_matrix=intergroup_mixing_matrix, token_rescale_factor=token_rescale_factor, gating_diagonal_matrix=gating_diagonal_matrix, expanding_diagonal_matrix=expanding_diagonal_matrix, contracting_diagonal_matrix=contracting_diagonal_matrix, feature_rescale_factor=feature_rescale_factor)


def rms_norm(values, gain):
    scale = lax.rsqrt(lax.optimization_barrier(jnp.mean(values * values, axis=-1, keepdims=True)) + 1e-06)
    return values * scale * gain.astype(jnp.float32)

def apply_encoder_level(operands):
    inflow, along, across, gain_one, gate_rows, up_rows, down_rows, gain_two = operands
    activation_vector = inflow.astype(jnp.float32)
    normed = rms_norm(activation_vector, gain_one).astype(jnp.bfloat16).reshape(B2, B1, D)
    mixed = jnp.einsum('aob,abc->aoc', along.astype(jnp.float32), normed.astype(jnp.float32)).astype(jnp.bfloat16)
    turned = jnp.einsum('oae,eoc->aoc', across.astype(jnp.float32), mixed.astype(jnp.float32)).astype(jnp.bfloat16)
    merged = activation_vector + turned.reshape(TOKENS, D).astype(jnp.float32)
    normed_mlp = rms_norm(merged, gain_two).astype(jnp.bfloat16).reshape(TOKENS, NB, D // NB)
    gate_proj = jnp.einsum('tkd,kdf->tkf', normed_mlp.astype(jnp.float32), gate_rows.reshape(NB, D // NB, FF // NB).astype(jnp.float32))
    up_proj = jnp.einsum('tkd,kdf->tkf', normed_mlp.astype(jnp.float32), up_rows.reshape(NB, D // NB, FF // NB).astype(jnp.float32))
    hidden = (jax.nn.silu(gate_proj) * up_proj).astype(jnp.bfloat16)
    lowered = jnp.einsum('tkf,kfe->tke', hidden.astype(jnp.float32), down_rows.reshape(NB, FF // NB, D // NB).astype(jnp.float32))
    return (merged + lowered.reshape(TOKENS, D)).astype(jnp.bfloat16)

def reference(pending_residual, intragroup_mixing_matrix, intergroup_mixing_matrix, token_rescale_factor, gating_diagonal_matrix, expanding_diagonal_matrix, contracting_diagonal_matrix, feature_rescale_factor):
    encoder_level_results = lax.map(apply_encoder_level, (pending_residual, intragroup_mixing_matrix, intergroup_mixing_matrix, token_rescale_factor, gating_diagonal_matrix, expanding_diagonal_matrix, contracting_diagonal_matrix, feature_rescale_factor))
    return jnp.roll(encoder_level_results, 1, axis=0)
```

```python
import functools

import jax
import jax.numpy as jnp
from jax import lax
from jax.experimental import pallas as pl
from jax.experimental.pallas import tpu as pltpu
from jax.sharding import PartitionSpec as P

NB = 4
B1 = 512
CHUNKS = 4
AHEAD = 2
EPS = 1e-06
MESH = pl.DeviceIdType.MESH


def layer_kernel(
    n, sections, D, FF,
    x_ref, a_ref, w_ref, g1_ref, gate_ref, up_ref, down_ref, g2_ref,
    out_ref,
    normed, mixed, xr, mr, w2, w3, wg, wu, wd, merged, st, outs,
    xs, xrs, ms, mrs, os_, ors, ws, wrs, ts, trs, vs, vrs,
):
    q = n // NB
    R = B1 // q
    r = R // CHUNKS
    FB, FH = D // NB, FF // NB
    own_offsets = B1 // n
    me = lax.axis_index("seq")
    sec = lax.axis_index("section")
    k, h = me // q, me % q
    after = (sec + 1) % sections
    before = (sec + sections - 1) % sections

    barrier = pltpu.get_barrier_semaphore()

    def greet(j, carry):
        pl.semaphore_signal(barrier, inc=1, device_id=(after, j), device_id_type=MESH)
        pl.semaphore_signal(barrier, inc=1, device_id=(before, j), device_id_type=MESH)
        return carry

    def greet_peer(d, carry):
        j = (me + d) % n
        pl.semaphore_signal(barrier, inc=1, device_id=(sec, j), device_id_type=MESH)
        return carry

    lax.fori_loop(1, n, greet_peer, 0)
    lax.fori_loop(0, n, greet, 0)

    def block_of(ref, c, j):
        rows = pl.multiple_of((j % q) * R + c * r, r)
        cols = pl.multiple_of((j // q) * FB, FB)
        return ref.at[pl.ds(rows, r), pl.ds(cols, FB)]

    def slot(ref, c, j):
        return ref.at[c, pl.ds(pl.multiple_of(j * r, r), r), :]

    def spread(src, land, send, recv, c, j):
        return pltpu.make_async_remote_copy(
            src_ref=block_of(src, c, j), dst_ref=slot(land, c, me),
            send_sem=send.at[c, j], recv_sem=recv.at[c, me],
            device_id=(sec, j), device_id_type=MESH,
        )

    def arrival(land, send, recv, c, j):
        return pltpu.make_async_remote_copy(
            src_ref=slot(land, c, j), dst_ref=slot(land, c, j),
            send_sem=send.at[c, j], recv_sem=recv.at[c, j],
            device_id=(sec, j), device_id_type=MESH,
        )

    def keep(src, land, recv, c):
        return pltpu.make_async_copy(block_of(src, c, me), slot(land, c, me), recv.at[c, me])

    def start_chunk(src, land, send, recv, c):
        def one(d, carry):
            spread(src, land, send, recv, c, (me + d) % n).start()
            return carry

        lax.fori_loop(1, n, one, 0)
        keep(src, land, recv, c).start()

    def await_chunk(src, land, send, recv, c):
        def one(d, carry):
            arrival(land, send, recv, c, (me + d) % n).wait_recv()
            return carry

        lax.fori_loop(1, n, one, 0)
        keep(src, land, recv, c).wait()

    weights = ((gate_ref, wg, FB // q), (up_ref, wu, FB // q), (down_ref, wd, FH // q))

    def weight_copy(i, d):
        src, land, rows = weights[i]
        j = k * q + (h + d) % q
        return pltpu.make_async_remote_copy(
            src_ref=src, dst_ref=land.at[pl.ds(pl.multiple_of(h * rows, rows), rows), :],
            send_sem=ws.at[i, (h + d) % q], recv_sem=wrs.at[i, h],
            device_id=(sec, j), device_id_type=MESH,
        )

    def weight_arrival(i, d):
        src, land, rows = weights[i]
        p = (h + d) % q
        view = land.at[pl.ds(pl.multiple_of(p * rows, rows), rows), :]
        return pltpu.make_async_remote_copy(
            src_ref=view, dst_ref=view, send_sem=ws.at[i, p], recv_sem=wrs.at[i, p],
            device_id=(sec, k * q + p), device_id_type=MESH,
        )

    def weight_keep(i):
        src, land, rows = weights[i]
        return pltpu.make_async_copy(
            src, land.at[pl.ds(pl.multiple_of(h * rows, rows), rows), :], wrs.at[i, h]
        )

    def across_view(i):
        return w2.at[pl.ds(pl.multiple_of(i * own_offsets, own_offsets), own_offsets), :]

    def across_copy(b):
        return pltpu.make_async_remote_copy(
            src_ref=w_ref, dst_ref=across_view(me % NB),
            send_sem=vs.at[b], recv_sem=vrs.at[me % NB],
            device_id=(sec, b * q + me // NB), device_id_type=MESH,
        )

    def across_arrival(i):
        return pltpu.make_async_remote_copy(
            src_ref=across_view(i), dst_ref=across_view(i),
            send_sem=vs.at[i], recv_sem=vrs.at[i],
            device_id=(sec, h * NB + i), device_id_type=MESH,
        )

    def across_keep():
        return pltpu.make_async_copy(w_ref, across_view(me % NB), vrs.at[me % NB])

    def stat_copy(c, d):
        b = (k + d) % NB
        return pltpu.make_async_remote_copy(
            src_ref=st.at[c, k], dst_ref=st.at[c, k],
            send_sem=ts.at[c, b], recv_sem=trs.at[c, k],
            device_id=(sec, b * q + h), device_id_type=MESH,
        )

    def stat_arrival(c, d):
        b = (k + d) % NB
        return pltpu.make_async_remote_copy(
            src_ref=st.at[c, b], dst_ref=st.at[c, b],
            send_sem=ts.at[c, b], recv_sem=trs.at[c, b],
            device_id=(sec, b * q + h), device_id_type=MESH,
        )

    def out_view(c, j):
        rows = pl.multiple_of((j % q) * R + c * r, r)
        cols = pl.multiple_of((j // q) * FB, FB)
        return out_ref.at[pl.ds(rows, r), pl.ds(cols, FB)]

    def out_copy(c, j):
        return pltpu.make_async_remote_copy(
            src_ref=slot(outs, c, j), dst_ref=out_view(c, me),
            send_sem=os_.at[c, j], recv_sem=ors.at[c, me],
            device_id=(after, j), device_id_type=MESH,
        )

    def out_arrival(c, j):
        return pltpu.make_async_remote_copy(
            src_ref=slot(outs, c, j), dst_ref=out_view(c, j),
            send_sem=os_.at[c, j], recv_sem=ors.at[c, j],
            device_id=(before, j), device_id_type=MESH,
        )

    pl.semaphore_wait(barrier, 3 * n - 1)

    for b in range(NB):
        to = b * q + me // NB

        @pl.when(to != me)
        def _():
            across_copy(b).start()

        @pl.when(to == me)
        def _():
            across_keep().start()

    start_chunk(x_ref, xr, xs, xrs, 0)

    def norm_rows(i, carry):
        rows = pl.ds(pl.multiple_of(i * 64, 64), 64)
        v = x_ref[rows, :].astype(jnp.float32)
        scale = lax.rsqrt(jnp.sum(v * v, axis=-1, keepdims=True) * (1.0 / D) + EPS)
        normed[rows, :] = (v * scale * g1_ref[...]).astype(jnp.bfloat16)
        return carry

    lax.fori_loop(0, B1 // 64, norm_rows, 0)
    for b in range(NB):
        cols = slice(b * FB, (b + 1) * FB)
        mixed[:, cols] = jnp.dot(
            a_ref[...], normed[:, cols], preferred_element_type=jnp.float32
        ).astype(jnp.bfloat16)

    start_chunk(mixed, mr, ms, mrs, 0)
    for i in range(3):
        for d in range(1, q):
            weight_copy(i, d).start()
        weight_keep(i).start()
    for c in range(1, AHEAD):
        start_chunk(mixed, mr, ms, mrs, c)
        start_chunk(x_ref, xr, xs, xrs, c)

    for i in range(NB):
        come = h * NB + i

        @pl.when(come != me)
        def _():
            across_arrival(i).wait_recv()

        @pl.when(come == me)
        def _():
            across_keep().wait()

    for a in range(n):
        w3[a] = w2[:, a * n : (a + 1) * n].astype(jnp.float32)

    T = 16

    def turn_tile(c, i):
        rows = pl.multiple_of(i * T, T)

        def piece(e):
            return pl.ds(pl.multiple_of(e * r + rows, T), T)

        def weights_of(a):
            return w3[a, pl.ds(pl.multiple_of(c * r + rows, T), T), :]

        def finish(a, acc):
            v = xr[c, piece(a), :].astype(jnp.float32)
            v = v + acc.astype(jnp.bfloat16).astype(jnp.float32)
            merged[c, piece(a), :] = v

        if n <= 8:
            m = [mr[c, piece(e), :].astype(jnp.float32) for e in range(n)]
            for a in range(n):
                w = weights_of(a)
                acc = w[:, 0:1] * m[0]
                for e in range(1, n):
                    acc = acc + w[:, e : e + 1] * m[e]
                finish(a, acc)
        else:

            def one(a, carry):
                w = weights_of(a)
                acc = jnp.zeros((T, FB), jnp.float32)
                for e in range(n):
                    acc = acc + w[:, e : e + 1] * mr[c, piece(e), :].astype(jnp.float32)
                finish(a, acc)
                return carry

            lax.fori_loop(0, n, one, 0)

    def step(c, carry):
        @pl.when(c < CHUNKS)
        def _():
            await_chunk(mixed, mr, ms, mrs, c)
            await_chunk(x_ref, xr, xs, xrs, c)

            def tile(i, carry):
                turn_tile(c, i)
                return carry

            lax.fori_loop(0, r // T, tile, 0)
            v = merged[c]
            st[c, k] = lax.dot_general(
                jnp.ones((8, FB), jnp.float32), v * v, (((1,), (1,)), ((), ())),
                precision=lax.Precision.HIGHEST, preferred_element_type=jnp.float32,
            )
            for d in range(1, NB):
                stat_copy(c, d).start()

        @pl.when(c + AHEAD < CHUNKS)
        def _():
            start_chunk(mixed, mr, ms, mrs, c + AHEAD)
            start_chunk(x_ref, xr, xs, xrs, c + AHEAD)

        @pl.when(c == 1)
        def _():
            for i in range(3):
                for d in range(1, q):
                    weight_arrival(i, d).wait_recv()
                weight_keep(i).wait()

        @pl.when(c >= 1)
        def _():
            p = c - 1
            for d in range(1, NB):
                stat_arrival(p, d).wait_recv()
            total = (st[p, 0] + st[p, 1]) + (st[p, 2] + st[p, 3])
            scale = jnp.transpose(lax.rsqrt(total * (1.0 / D) + EPS))[:, 0:1]
            half = n * r // 2
            for t in range(2):
                rows = slice(t * half, (t + 1) * half)
                v = merged[p, rows, :]
                inner = (v * scale[rows] * g2_ref[...]).astype(jnp.bfloat16)
                gate = jnp.dot(inner, wg[...], preferred_element_type=jnp.float32)
                up = jnp.dot(inner, wu[...], preferred_element_type=jnp.float32)
                hidden = (gate / (1.0 + jnp.exp(-gate)) * up).astype(jnp.bfloat16)
                low = jnp.dot(hidden, wd[...], preferred_element_type=jnp.float32)
                outs[p, rows, :] = (v + low).astype(jnp.bfloat16)

            def one(d, carry):
                out_copy(p, (me + d) % n).start()
                return carry

            lax.fori_loop(0, n, one, 0)

        return carry

    lax.fori_loop(0, CHUNKS + 1, step, 0)

    for b in range(NB):

        @pl.when(b * q + me // NB != me)
        def _():
            across_copy(b).wait_send()

    for i in range(3):
        for d in range(1, q):
            weight_copy(i, d).wait_send()

    def drain(c, carry):
        def one(d, carry):
            j = (me + d) % n
            spread(x_ref, xr, xs, xrs, c, j).wait_send()
            spread(mixed, mr, ms, mrs, c, j).wait_send()
            return carry

        lax.fori_loop(1, n, one, 0)
        for d in range(1, NB):
            stat_copy(c, d).wait_send()

        def last(j, carry):
            out_copy(c, j).wait_send()
            out_arrival(c, j).wait_recv()
            return carry

        return lax.fori_loop(0, n, last, carry)

    lax.fori_loop(0, CHUNKS, drain, 0)


def shards(n, sections, pending, along, across, gain_one, gate, up, down, gain_two):
    D = pending.shape[2]
    FB = D // NB
    FH = gate.shape[2]
    FF = FH * NB
    q = n // NB
    R = B1 // q
    r = R // CHUNKS
    flat = across[0].reshape(B1 // n, n * n)
    lanes = max(n * n, 128)
    flat = jnp.pad(flat, ((0, 0), (0, lanes - n * n)))
    k = lax.axis_index("seq") // q
    gain_two = lax.dynamic_slice(gain_two, (0, k * FB), (1, FB))
    vmem = pl.BlockSpec(memory_space=pltpu.VMEM)
    anywhere = pl.BlockSpec(memory_space=pl.ANY)
    dma = pltpu.SemaphoreType.DMA
    bf, f32 = jnp.bfloat16, jnp.float32
    out = pl.pallas_call(
        functools.partial(layer_kernel, n, sections, D, FF),
        out_shape=jax.ShapeDtypeStruct((B1, D), bf),
        in_specs=[vmem, vmem, anywhere, vmem, anywhere, anywhere, anywhere, vmem],
        out_specs=anywhere,
        scratch_shapes=[
            pltpu.VMEM((B1, D), bf),
            pltpu.VMEM((B1, D), bf),
            pltpu.VMEM((CHUNKS, n * r, FB), bf),
            pltpu.VMEM((CHUNKS, n * r, FB), bf),
            pltpu.VMEM((R, lanes), bf),
            pltpu.VMEM((n, R, n), f32),
            pltpu.VMEM((FB, FH), bf),
            pltpu.VMEM((FB, FH), bf),
            pltpu.VMEM((FH, FB), bf),
            pltpu.VMEM((CHUNKS, n * r, FB), f32),
            pltpu.VMEM((CHUNKS, NB, 8, n * r), f32),
            pltpu.VMEM((CHUNKS, n * r, FB), bf),
            dma((CHUNKS, n)), dma((CHUNKS, n)),
            dma((CHUNKS, n)), dma((CHUNKS, n)),
            dma((CHUNKS, n)), dma((CHUNKS, n)),
            dma((3, q)), dma((3, q)),
            dma((CHUNKS, NB)), dma((CHUNKS, NB)),
            dma((NB,)), dma((NB,)),
        ],
        compiler_params=pltpu.CompilerParams(
            collective_id=0, has_side_effects=True, vmem_limit_bytes=48 * 1024 * 1024
        ),
        name="encoder_layer",
    )(pending[0], along[0, 0], flat, gain_one, gate[0], up[0], down[0], gain_two)
    return out[None]


def solution(mesh):
    return jax.shard_map(
        functools.partial(shards, mesh.shape["seq"], mesh.shape["section"]),
        mesh=mesh,
        in_specs=(
            P("section", "seq", None),
            P("section", "seq", None, None),
            P("section", "seq", None, None),
            P("section", None),
            P("section", "seq", None),
            P("section", "seq", None),
            P("section", "seq", None),
            P("section", None),
        ),
        out_specs=P("section", "seq", None),
        check_vma=False,
    )
```

```python
import functools

import jax
import jax.numpy as jnp
from jax import lax
from jax.experimental import pallas as pl
from jax.experimental.pallas import tpu as pltpu
from jax.sharding import PartitionSpec as P

NB = 4
B1 = 512
CHUNKS = 4
AHEAD = 2
EPS = 1e-06
MESH = pl.DeviceIdType.MESH


def layer_kernel(
    n, sections, D, FF,
    x_in, a_in, w_ref, g1_in, gate_ref, up_ref, down_ref, g2_in,
    out_ref,
    x_ref, a_ref, g1_ref, g2_ref, ls,
    normed, mixed, xr, mr, w2, w3, wg, wu, wd, merged, st, outs,
    xs, xrs, ms, mrs, os_, ors, ws, wrs, ts, trs, vs, vrs,
):
    q = n // NB
    R = B1 // q
    r = R // CHUNKS
    FB, FH = D // NB, FF // NB
    own_offsets = B1 // n
    me = lax.axis_index("seq")
    sec = lax.axis_index("section")
    k, h = me // q, me % q
    after = (sec + 1) % sections
    before = (sec + sections - 1) % sections

    loads = [
        pltpu.make_async_copy(x_in, x_ref, ls.at[0]),
        pltpu.make_async_copy(a_in, a_ref, ls.at[1]),
        pltpu.make_async_copy(g1_in, g1_ref, ls.at[2]),
        pltpu.make_async_copy(
            g2_in.at[:, pl.ds(pl.multiple_of(k * FB, FB), FB)], g2_ref, ls.at[3]
        ),
    ]
    for load in loads:
        load.start()

    barrier = pltpu.get_barrier_semaphore()

    def greet(j, carry):
        pl.semaphore_signal(barrier, inc=1, device_id=(after, j), device_id_type=MESH)
        pl.semaphore_signal(barrier, inc=1, device_id=(before, j), device_id_type=MESH)
        return carry

    def greet_peer(d, carry):
        j = (me + d) % n
        pl.semaphore_signal(barrier, inc=1, device_id=(sec, j), device_id_type=MESH)
        return carry

    lax.fori_loop(1, n, greet_peer, 0)
    lax.fori_loop(0, n, greet, 0)

    def block_of(ref, c, j):
        rows = pl.multiple_of((j % q) * R + c * r, r)
        cols = pl.multiple_of((j // q) * FB, FB)
        return ref.at[pl.ds(rows, r), pl.ds(cols, FB)]

    def slot(ref, c, j):
        return ref.at[c, pl.ds(pl.multiple_of(j * r, r), r), :]

    def spread(src, land, send, recv, c, j):
        return pltpu.make_async_remote_copy(
            src_ref=block_of(src, c, j), dst_ref=slot(land, c, me),
            send_sem=send.at[c, j], recv_sem=recv.at[c, me],
            device_id=(sec, j), device_id_type=MESH,
        )

    def arrival(land, send, recv, c, j):
        return pltpu.make_async_remote_copy(
            src_ref=slot(land, c, j), dst_ref=slot(land, c, j),
            send_sem=send.at[c, j], recv_sem=recv.at[c, j],
            device_id=(sec, j), device_id_type=MESH,
        )

    def keep(src, land, recv, c):
        return pltpu.make_async_copy(block_of(src, c, me), slot(land, c, me), recv.at[c, me])

    def start_chunk(src, land, send, recv, c):
        def one(d, carry):
            spread(src, land, send, recv, c, (me + d) % n).start()
            return carry

        lax.fori_loop(1, n, one, 0)
        keep(src, land, recv, c).start()

    def await_chunk(src, land, send, recv, c):
        def one(d, carry):
            arrival(land, send, recv, c, (me + d) % n).wait_recv()
            return carry

        lax.fori_loop(1, n, one, 0)
        keep(src, land, recv, c).wait()

    weights = ((gate_ref, wg, FB // q), (up_ref, wu, FB // q), (down_ref, wd, FH // q))

    def weight_copy(i, d):
        src, land, rows = weights[i]
        j = k * q + (h + d) % q
        return pltpu.make_async_remote_copy(
            src_ref=src, dst_ref=land.at[pl.ds(pl.multiple_of(h * rows, rows), rows), :],
            send_sem=ws.at[i, (h + d) % q], recv_sem=wrs.at[i, h],
            device_id=(sec, j), device_id_type=MESH,
        )

    def weight_arrival(i, d):
        src, land, rows = weights[i]
        p = (h + d) % q
        view = land.at[pl.ds(pl.multiple_of(p * rows, rows), rows), :]
        return pltpu.make_async_remote_copy(
            src_ref=view, dst_ref=view, send_sem=ws.at[i, p], recv_sem=wrs.at[i, p],
            device_id=(sec, k * q + p), device_id_type=MESH,
        )

    def weight_keep(i):
        src, land, rows = weights[i]
        return pltpu.make_async_copy(
            src, land.at[pl.ds(pl.multiple_of(h * rows, rows), rows), :], wrs.at[i, h]
        )

    def across_view(i):
        return w2.at[pl.ds(pl.multiple_of(i * own_offsets, own_offsets), own_offsets), :]

    def across_copy(b):
        return pltpu.make_async_remote_copy(
            src_ref=w_ref, dst_ref=across_view(me % NB),
            send_sem=vs.at[b], recv_sem=vrs.at[me % NB],
            device_id=(sec, b * q + me // NB), device_id_type=MESH,
        )

    def across_arrival(i):
        return pltpu.make_async_remote_copy(
            src_ref=across_view(i), dst_ref=across_view(i),
            send_sem=vs.at[i], recv_sem=vrs.at[i],
            device_id=(sec, h * NB + i), device_id_type=MESH,
        )

    def across_keep():
        return pltpu.make_async_copy(w_ref, across_view(me % NB), vrs.at[me % NB])

    def stat_copy(c, d):
        b = (k + d) % NB
        return pltpu.make_async_remote_copy(
            src_ref=st.at[c, k], dst_ref=st.at[c, k],
            send_sem=ts.at[c, b], recv_sem=trs.at[c, k],
            device_id=(sec, b * q + h), device_id_type=MESH,
        )

    def stat_arrival(c, d):
        b = (k + d) % NB
        return pltpu.make_async_remote_copy(
            src_ref=st.at[c, b], dst_ref=st.at[c, b],
            send_sem=ts.at[c, b], recv_sem=trs.at[c, b],
            device_id=(sec, b * q + h), device_id_type=MESH,
        )

    def out_view(c, j):
        rows = pl.multiple_of((j % q) * R + c * r, r)
        cols = pl.multiple_of((j // q) * FB, FB)
        return out_ref.at[pl.ds(rows, r), pl.ds(cols, FB)]

    def out_copy(c, j):
        return pltpu.make_async_remote_copy(
            src_ref=slot(outs, c, j), dst_ref=out_view(c, me),
            send_sem=os_.at[c, j], recv_sem=ors.at[c, me],
            device_id=(after, j), device_id_type=MESH,
        )

    def out_arrival(c, j):
        return pltpu.make_async_remote_copy(
            src_ref=slot(outs, c, j), dst_ref=out_view(c, j),
            send_sem=os_.at[c, j], recv_sem=ors.at[c, j],
            device_id=(before, j), device_id_type=MESH,
        )

    pl.semaphore_wait(barrier, 3 * n - 1)
    for load in loads:
        load.wait()

    for b in range(NB):
        to = b * q + me // NB

        @pl.when(to != me)
        def _():
            across_copy(b).start()

        @pl.when(to == me)
        def _():
            across_keep().start()

    start_chunk(x_ref, xr, xs, xrs, 0)

    def norm_rows(i, carry):
        rows = pl.ds(pl.multiple_of(i * 64, 64), 64)
        v = x_ref[rows, :].astype(jnp.float32)
        scale = lax.rsqrt(jnp.sum(v * v, axis=-1, keepdims=True) * (1.0 / D) + EPS)
        normed[rows, :] = (v * scale * g1_ref[...]).astype(jnp.bfloat16)
        return carry

    lax.fori_loop(0, B1 // 64, norm_rows, 0)
    for b in range(NB):
        cols = slice(b * FB, (b + 1) * FB)
        mixed[:, cols] = jnp.dot(
            a_ref[...], normed[:, cols], preferred_element_type=jnp.float32
        ).astype(jnp.bfloat16)

    start_chunk(mixed, mr, ms, mrs, 0)
    for i in range(3):
        for d in range(1, q):
            weight_copy(i, d).start()
        weight_keep(i).start()
    for c in range(1, AHEAD):
        start_chunk(mixed, mr, ms, mrs, c)
        start_chunk(x_ref, xr, xs, xrs, c)

    for i in range(NB):
        come = h * NB + i

        @pl.when(come != me)
        def _():
            across_arrival(i).wait_recv()

        @pl.when(come == me)
        def _():
            across_keep().wait()

    for a in range(n):
        w3[a] = w2[:, a * n : (a + 1) * n].astype(jnp.float32)

    T = 16

    def turn_tile(c, i):
        rows = pl.multiple_of(i * T, T)

        def piece(e):
            return pl.ds(pl.multiple_of(e * r + rows, T), T)

        def weights_of(a):
            return w3[a, pl.ds(pl.multiple_of(c * r + rows, T), T), :]

        def finish(a, acc):
            v = xr[c, piece(a), :].astype(jnp.float32)
            v = v + acc.astype(jnp.bfloat16).astype(jnp.float32)
            merged[c, piece(a), :] = v

        if n <= 8:
            m = [mr[c, piece(e), :].astype(jnp.float32) for e in range(n)]
            for a in range(n):
                w = weights_of(a)
                acc = w[:, 0:1] * m[0]
                for e in range(1, n):
                    acc = acc + w[:, e : e + 1] * m[e]
                finish(a, acc)
        else:

            def one(a, carry):
                w = weights_of(a)
                acc = jnp.zeros((T, FB), jnp.float32)
                for e in range(n):
                    acc = acc + w[:, e : e + 1] * mr[c, piece(e), :].astype(jnp.float32)
                finish(a, acc)
                return carry

            lax.fori_loop(0, n, one, 0)

    def step(c, carry):
        @pl.when(c < CHUNKS)
        def _():
            await_chunk(mixed, mr, ms, mrs, c)
            await_chunk(x_ref, xr, xs, xrs, c)

            def tile(i, carry):
                turn_tile(c, i)
                return carry

            lax.fori_loop(0, r // T, tile, 0)
            v = merged[c]
            sums = lax.dot_general(
                jnp.ones((8, FB), jnp.float32), v * v, (((1,), (1,)), ((), ())),
                precision=lax.Precision.HIGHEST, preferred_element_type=jnp.float32,
            )
            st[c, k] = sums[0:1]
            for d in range(1, NB):
                stat_copy(c, d).start()

        @pl.when(c + AHEAD < CHUNKS)
        def _():
            start_chunk(mixed, mr, ms, mrs, c + AHEAD)
            start_chunk(x_ref, xr, xs, xrs, c + AHEAD)

        @pl.when(c == 1)
        def _():
            for i in range(3):
                for d in range(1, q):
                    weight_arrival(i, d).wait_recv()
                weight_keep(i).wait()

        @pl.when(c >= 1)
        def _():
            p = c - 1
            for d in range(1, NB):
                stat_arrival(p, d).wait_recv()
            total = (st[p, 0] + st[p, 1]) + (st[p, 2] + st[p, 3])
            scale = lax.rsqrt(total * (1.0 / D) + EPS)
            scale = jnp.transpose(jnp.broadcast_to(scale, (8, n * r)))[:, 0:1]
            half = n * r // 2
            for t in range(2):
                rows = slice(t * half, (t + 1) * half)
                v = merged[p, rows, :]
                inner = (v * scale[rows] * g2_ref[...]).astype(jnp.bfloat16)
                gate = jnp.dot(inner, wg[...], preferred_element_type=jnp.float32)
                up = jnp.dot(inner, wu[...], preferred_element_type=jnp.float32)
                hidden = (gate / (1.0 + jnp.exp(-gate)) * up).astype(jnp.bfloat16)
                low = jnp.dot(hidden, wd[...], preferred_element_type=jnp.float32)
                outs[p, rows, :] = (v + low).astype(jnp.bfloat16)

            def one(d, carry):
                out_copy(p, (me + d) % n).start()
                return carry

            lax.fori_loop(0, n, one, 0)

        return carry

    lax.fori_loop(0, CHUNKS + 1, step, 0)

    for b in range(NB):

        @pl.when(b * q + me // NB != me)
        def _():
            across_copy(b).wait_send()

    for i in range(3):
        for d in range(1, q):
            weight_copy(i, d).wait_send()

    def drain(c, carry):
        def one(d, carry):
            j = (me + d) % n
            spread(x_ref, xr, xs, xrs, c, j).wait_send()
            spread(mixed, mr, ms, mrs, c, j).wait_send()
            return carry

        lax.fori_loop(1, n, one, 0)
        for d in range(1, NB):
            stat_copy(c, d).wait_send()

        def last(j, carry):
            out_copy(c, j).wait_send()
            out_arrival(c, j).wait_recv()
            return carry

        return lax.fori_loop(0, n, last, carry)

    lax.fori_loop(0, CHUNKS, drain, 0)


def shards(n, sections, pending, along, across, gain_one, gate, up, down, gain_two):
    D = pending.shape[2]
    FB = D // NB
    FH = gate.shape[2]
    FF = FH * NB
    q = n // NB
    R = B1 // q
    r = R // CHUNKS
    flat = across[0].reshape(B1 // n, n * n)
    lanes = max(n * n, 128)
    flat = jnp.pad(flat, ((0, 0), (0, lanes - n * n)))
    anywhere = pl.BlockSpec(memory_space=pl.ANY)
    dma = pltpu.SemaphoreType.DMA
    bf, f32 = jnp.bfloat16, jnp.float32
    out = pl.pallas_call(
        functools.partial(layer_kernel, n, sections, D, FF),
        out_shape=jax.ShapeDtypeStruct((B1, D), bf),
        in_specs=[anywhere] * 8,
        out_specs=anywhere,
        scratch_shapes=[
            pltpu.VMEM((B1, D), bf),
            pltpu.VMEM((B1, B1), bf),
            pltpu.VMEM((1, D), f32),
            pltpu.VMEM((1, FB), f32),
            dma((4,)),
            pltpu.VMEM((B1, D), bf),
            pltpu.VMEM((B1, D), bf),
            pltpu.VMEM((CHUNKS, n * r, FB), bf),
            pltpu.VMEM((CHUNKS, n * r, FB), bf),
            pltpu.VMEM((R, lanes), bf),
            pltpu.VMEM((n, R, n), f32),
            pltpu.VMEM((FB, FH), bf),
            pltpu.VMEM((FB, FH), bf),
            pltpu.VMEM((FH, FB), bf),
            pltpu.VMEM((CHUNKS, n * r, FB), f32),
            pltpu.VMEM((CHUNKS, NB, 1, n * r), f32),
            pltpu.VMEM((CHUNKS, n * r, FB), bf),
            dma((CHUNKS, n)), dma((CHUNKS, n)),
            dma((CHUNKS, n)), dma((CHUNKS, n)),
            dma((CHUNKS, n)), dma((CHUNKS, n)),
            dma((3, q)), dma((3, q)),
            dma((CHUNKS, NB)), dma((CHUNKS, NB)),
            dma((NB,)), dma((NB,)),
        ],
        compiler_params=pltpu.CompilerParams(
            collective_id=0, has_side_effects=True, vmem_limit_bytes=60 * 1024 * 1024
        ),
        name="encoder_layer",
    )(pending[0], along[0, 0], flat, gain_one, gate[0], up[0], down[0], gain_two)
    return out[None]


def solution(mesh):
    return jax.shard_map(
        functools.partial(shards, mesh.shape["seq"], mesh.shape["section"]),
        mesh=mesh,
        in_specs=(
            P("section", "seq", None),
            P("section", "seq", None, None),
            P("section", "seq", None, None),
            P("section", None),
            P("section", "seq", None),
            P("section", "seq", None),
            P("section", "seq", None),
            P("section", None),
        ),
        out_specs=P("section", "seq", None),
        check_vma=False,
    )
```

```python
import functools

import jax
import jax.numpy as jnp
from jax import lax
from jax.experimental import pallas as pl
from jax.experimental.pallas import tpu as pltpu
from jax.sharding import PartitionSpec as P

NB = 4
B1 = 512
CHUNKS = 4
AHEAD = 2
EPS = 1e-06
MESH = pl.DeviceIdType.MESH


def layer_kernel(
    n, sections, D, FF,
    x_in, a_in, w_ref, g1_in, gate_ref, up_ref, down_ref, g2_in,
    out_ref,
    x_ref, a_ref, g1_ref, g2_ref, ls,
    normed, mixed, xr, mr, w2, w3, wg, wu, wd, merged, st, outs,
    xs, xrs, ms, mrs, os_, ors, ws, wrs, ts, trs, vs, vrs,
):
    q = n // NB
    R = B1 // q
    r = R // CHUNKS
    FB, FH = D // NB, FF // NB
    own_offsets = B1 // n
    me = lax.axis_index("seq")
    sec = lax.axis_index("section")
    k, h = me // q, me % q
    after = (sec + 1) % sections
    before = (sec + sections - 1) % sections

    loads = [
        pltpu.make_async_copy(x_in, x_ref, ls.at[0]),
        pltpu.make_async_copy(a_in, a_ref, ls.at[1]),
        pltpu.make_async_copy(g1_in, g1_ref, ls.at[2]),
        pltpu.make_async_copy(
            g2_in.at[:, pl.ds(pl.multiple_of(k * FB, FB), FB)], g2_ref, ls.at[3]
        ),
    ]
    for load in loads:
        load.start()

    barrier = pltpu.get_barrier_semaphore()

    def greet(j, carry):
        pl.semaphore_signal(barrier, inc=1, device_id=(after, j), device_id_type=MESH)
        pl.semaphore_signal(barrier, inc=1, device_id=(before, j), device_id_type=MESH)
        return carry

    def greet_peer(d, carry):
        j = (me + d) % n
        pl.semaphore_signal(barrier, inc=1, device_id=(sec, j), device_id_type=MESH)
        return carry

    lax.fori_loop(1, n, greet_peer, 0)
    lax.fori_loop(0, n, greet, 0)

    def block_of(ref, c, j):
        rows = pl.multiple_of((j % q) * R + c * r, r)
        cols = pl.multiple_of((j // q) * FB, FB)
        return ref.at[pl.ds(rows, r), pl.ds(cols, FB)]

    def slot(ref, c, j):
        return ref.at[c, pl.ds(pl.multiple_of(j * r, r), r), :]

    def spread(src, land, send, recv, c, j):
        return pltpu.make_async_remote_copy(
            src_ref=block_of(src, c, j), dst_ref=slot(land, c, me),
            send_sem=send.at[c, j], recv_sem=recv.at[c, me],
            device_id=(sec, j), device_id_type=MESH,
        )

    def arrival(land, send, recv, c, j):
        return pltpu.make_async_remote_copy(
            src_ref=slot(land, c, j), dst_ref=slot(land, c, j),
            send_sem=send.at[c, j], recv_sem=recv.at[c, j],
            device_id=(sec, j), device_id_type=MESH,
        )

    def keep(src, land, recv, c):
        return pltpu.make_async_copy(block_of(src, c, me), slot(land, c, me), recv.at[c, me])

    def start_chunk(src, land, send, recv, c):
        for dk in (2, 1, 3, 0):

            def one(dh, carry):
                j = (k + dk) % NB * q + (h + dh) % q
                spread(src, land, send, recv, c, j).start()
                return carry

            lax.fori_loop(1 if dk == 0 else 0, q, one, 0)

        keep(src, land, recv, c).start()

    def await_chunk(src, land, send, recv, c):
        def one(d, carry):
            arrival(land, send, recv, c, (me + d) % n).wait_recv()
            return carry

        lax.fori_loop(1, n, one, 0)
        keep(src, land, recv, c).wait()

    weights = ((gate_ref, wg, FB // q), (up_ref, wu, FB // q), (down_ref, wd, FH // q))

    def weight_copy(i, d):
        src, land, rows = weights[i]
        j = k * q + (h + d) % q
        return pltpu.make_async_remote_copy(
            src_ref=src, dst_ref=land.at[pl.ds(pl.multiple_of(h * rows, rows), rows), :],
            send_sem=ws.at[i, (h + d) % q], recv_sem=wrs.at[i, h],
            device_id=(sec, j), device_id_type=MESH,
        )

    def weight_arrival(i, d):
        src, land, rows = weights[i]
        p = (h + d) % q
        view = land.at[pl.ds(pl.multiple_of(p * rows, rows), rows), :]
        return pltpu.make_async_remote_copy(
            src_ref=view, dst_ref=view, send_sem=ws.at[i, p], recv_sem=wrs.at[i, p],
            device_id=(sec, k * q + p), device_id_type=MESH,
        )

    def weight_keep(i):
        src, land, rows = weights[i]
        return pltpu.make_async_copy(
            src, land.at[pl.ds(pl.multiple_of(h * rows, rows), rows), :], wrs.at[i, h]
        )

    def across_view(i):
        return w2.at[pl.ds(pl.multiple_of(i * own_offsets, own_offsets), own_offsets), :]

    def across_copy(b):
        return pltpu.make_async_remote_copy(
            src_ref=w_ref, dst_ref=across_view(me % NB),
            send_sem=vs.at[b], recv_sem=vrs.at[me % NB],
            device_id=(sec, b * q + me // NB), device_id_type=MESH,
        )

    def across_arrival(i):
        return pltpu.make_async_remote_copy(
            src_ref=across_view(i), dst_ref=across_view(i),
            send_sem=vs.at[i], recv_sem=vrs.at[i],
            device_id=(sec, h * NB + i), device_id_type=MESH,
        )

    def across_keep():
        return pltpu.make_async_copy(w_ref, across_view(me % NB), vrs.at[me % NB])

    def stat_copy(c, d):
        b = (k + d) % NB
        return pltpu.make_async_remote_copy(
            src_ref=st.at[c, k], dst_ref=st.at[c, k],
            send_sem=ts.at[c, b], recv_sem=trs.at[c, k],
            device_id=(sec, b * q + h), device_id_type=MESH,
        )

    def stat_arrival(c, d):
        b = (k + d) % NB
        return pltpu.make_async_remote_copy(
            src_ref=st.at[c, b], dst_ref=st.at[c, b],
            send_sem=ts.at[c, b], recv_sem=trs.at[c, b],
            device_id=(sec, b * q + h), device_id_type=MESH,
        )

    def out_view(c, j):
        rows = pl.multiple_of((j % q) * R + c * r, r)
        cols = pl.multiple_of((j // q) * FB, FB)
        return out_ref.at[pl.ds(rows, r), pl.ds(cols, FB)]

    def out_copy(c, j):
        return pltpu.make_async_remote_copy(
            src_ref=slot(outs, c, j), dst_ref=out_view(c, me),
            send_sem=os_.at[c, j], recv_sem=ors.at[c, me],
            device_id=(after, j), device_id_type=MESH,
        )

    def out_arrival(c, j):
        return pltpu.make_async_remote_copy(
            src_ref=slot(outs, c, j), dst_ref=out_view(c, j),
            send_sem=os_.at[c, j], recv_sem=ors.at[c, j],
            device_id=(before, j), device_id_type=MESH,
        )

    pl.semaphore_wait(barrier, 3 * n - 1)
    for b in range(NB):
        to = b * q + me // NB

        @pl.when(to != me)
        def _():
            across_copy(b).start()

        @pl.when(to == me)
        def _():
            across_keep().start()

    start_chunk(x_in, xr, xs, xrs, 0)

    for load in loads:
        load.wait()

    def norm_rows(i, carry):
        rows = pl.ds(pl.multiple_of(i * 64, 64), 64)
        v = x_ref[rows, :].astype(jnp.float32)
        scale = lax.rsqrt(jnp.sum(v * v, axis=-1, keepdims=True) * (1.0 / D) + EPS)
        normed[rows, :] = (v * scale * g1_ref[...]).astype(jnp.bfloat16)
        return carry

    lax.fori_loop(0, B1 // 64, norm_rows, 0)
    for b in range(NB):
        cols = slice(b * FB, (b + 1) * FB)
        mixed[:, cols] = jnp.dot(
            a_ref[...], normed[:, cols], preferred_element_type=jnp.float32
        ).astype(jnp.bfloat16)

    start_chunk(mixed, mr, ms, mrs, 0)
    for i in range(3):
        for d in range(1, q):
            weight_copy(i, d).start()
        weight_keep(i).start()
    for c in range(1, AHEAD):
        start_chunk(mixed, mr, ms, mrs, c)
        start_chunk(x_in, xr, xs, xrs, c)

    for i in range(NB):
        come = h * NB + i

        @pl.when(come != me)
        def _():
            across_arrival(i).wait_recv()

        @pl.when(come == me)
        def _():
            across_keep().wait()

    for a in range(n):
        w3[a] = w2[:, a * n : (a + 1) * n].astype(jnp.float32)

    T = 16

    def turn_tile(c, i):
        rows = pl.multiple_of(i * T, T)

        def piece(e):
            return pl.ds(pl.multiple_of(e * r + rows, T), T)

        def weights_of(a):
            return w3[a, pl.ds(pl.multiple_of(c * r + rows, T), T), :]

        def finish(a, acc):
            v = xr[c, piece(a), :].astype(jnp.float32)
            v = v + acc.astype(jnp.bfloat16).astype(jnp.float32)
            merged[c, piece(a), :] = v

        if n <= 8:
            m = [mr[c, piece(e), :].astype(jnp.float32) for e in range(n)]
            for a in range(n):
                w = weights_of(a)
                acc = w[:, 0:1] * m[0]
                for e in range(1, n):
                    acc = acc + w[:, e : e + 1] * m[e]
                finish(a, acc)
        else:

            def one(a, carry):
                w = weights_of(a)
                acc = jnp.zeros((T, FB), jnp.float32)
                for e in range(n):
                    acc = acc + w[:, e : e + 1] * mr[c, piece(e), :].astype(jnp.float32)
                finish(a, acc)
                return carry

            lax.fori_loop(0, n, one, 0)

    def step(c, carry):
        @pl.when(c < CHUNKS)
        def _():
            await_chunk(mixed, mr, ms, mrs, c)
            await_chunk(x_in, xr, xs, xrs, c)

            def tile(i, carry):
                turn_tile(c, i)
                return carry

            lax.fori_loop(0, r // T, tile, 0)
            v = merged[c]
            sums = lax.dot_general(
                jnp.ones((8, FB), jnp.float32), v * v, (((1,), (1,)), ((), ())),
                precision=lax.Precision.HIGHEST, preferred_element_type=jnp.float32,
            )
            st[c, k] = sums[0:1]
            for d in range(1, NB):
                stat_copy(c, d).start()

        @pl.when(c + AHEAD < CHUNKS)
        def _():
            start_chunk(mixed, mr, ms, mrs, c + AHEAD)
            start_chunk(x_in, xr, xs, xrs, c + AHEAD)

        @pl.when(c == 1)
        def _():
            for i in range(3):
                for d in range(1, q):
                    weight_arrival(i, d).wait_recv()
                weight_keep(i).wait()

        @pl.when(c >= 1)
        def _():
            p = c - 1
            for d in range(1, NB):
                stat_arrival(p, d).wait_recv()
            total = (st[p, 0] + st[p, 1]) + (st[p, 2] + st[p, 3])
            scale = lax.rsqrt(total * (1.0 / D) + EPS)
            scale = jnp.transpose(jnp.broadcast_to(scale, (8, n * r)))[:, 0:1]
            half = n * r // 2
            for t in range(2):
                rows = slice(t * half, (t + 1) * half)
                v = merged[p, rows, :]
                inner = (v * scale[rows] * g2_ref[...]).astype(jnp.bfloat16)
                gate = jnp.dot(inner, wg[...], preferred_element_type=jnp.float32)
                up = jnp.dot(inner, wu[...], preferred_element_type=jnp.float32)
                hidden = (gate / (1.0 + jnp.exp(-gate)) * up).astype(jnp.bfloat16)
                low = jnp.dot(hidden, wd[...], preferred_element_type=jnp.float32)
                outs[p, rows, :] = (v + low).astype(jnp.bfloat16)

            def one(d, carry):
                out_copy(p, (me + d) % n).start()
                return carry

            lax.fori_loop(0, n, one, 0)

        return carry

    lax.fori_loop(0, CHUNKS + 1, step, 0)

    for b in range(NB):

        @pl.when(b * q + me // NB != me)
        def _():
            across_copy(b).wait_send()

    for i in range(3):
        for d in range(1, q):
            weight_copy(i, d).wait_send()

    def drain(c, carry):
        def one(d, carry):
            j = (me + d) % n
            spread(x_in, xr, xs, xrs, c, j).wait_send()
            spread(mixed, mr, ms, mrs, c, j).wait_send()
            return carry

        lax.fori_loop(1, n, one, 0)
        for d in range(1, NB):
            stat_copy(c, d).wait_send()

        def last(j, carry):
            out_copy(c, j).wait_send()
            out_arrival(c, j).wait_recv()
            return carry

        return lax.fori_loop(0, n, last, carry)

    lax.fori_loop(0, CHUNKS, drain, 0)


def shards(n, sections, pending, along, across, gain_one, gate, up, down, gain_two):
    D = pending.shape[2]
    FB = D // NB
    FH = gate.shape[2]
    FF = FH * NB
    q = n // NB
    R = B1 // q
    r = R // CHUNKS
    flat = across[0].reshape(B1 // n, n * n)
    lanes = max(n * n, 128)
    flat = jnp.pad(flat, ((0, 0), (0, lanes - n * n)))
    anywhere = pl.BlockSpec(memory_space=pl.ANY)
    dma = pltpu.SemaphoreType.DMA
    bf, f32 = jnp.bfloat16, jnp.float32
    out = pl.pallas_call(
        functools.partial(layer_kernel, n, sections, D, FF),
        out_shape=jax.ShapeDtypeStruct((B1, D), bf),
        in_specs=[anywhere] * 8,
        out_specs=anywhere,
        scratch_shapes=[
            pltpu.VMEM((B1, D), bf),
            pltpu.VMEM((B1, B1), bf),
            pltpu.VMEM((1, D), f32),
            pltpu.VMEM((1, FB), f32),
            dma((4,)),
            pltpu.VMEM((B1, D), bf),
            pltpu.VMEM((B1, D), bf),
            pltpu.VMEM((CHUNKS, n * r, FB), bf),
            pltpu.VMEM((CHUNKS, n * r, FB), bf),
            pltpu.VMEM((R, lanes), bf),
            pltpu.VMEM((n, R, n), f32),
            pltpu.VMEM((FB, FH), bf),
            pltpu.VMEM((FB, FH), bf),
            pltpu.VMEM((FH, FB), bf),
            pltpu.VMEM((CHUNKS, n * r, FB), f32),
            pltpu.VMEM((CHUNKS, NB, 1, n * r), f32),
            pltpu.VMEM((CHUNKS, n * r, FB), bf),
            dma((CHUNKS, n)), dma((CHUNKS, n)),
            dma((CHUNKS, n)), dma((CHUNKS, n)),
            dma((CHUNKS, n)), dma((CHUNKS, n)),
            dma((3, q)), dma((3, q)),
            dma((CHUNKS, NB)), dma((CHUNKS, NB)),
            dma((NB,)), dma((NB,)),
        ],
        compiler_params=pltpu.CompilerParams(
            collective_id=0, has_side_effects=True, vmem_limit_bytes=60 * 1024 * 1024
        ),
        name="encoder_layer",
    )(pending[0], along[0, 0], flat, gain_one, gate[0], up[0], down[0], gain_two)
    return out[None]


def solution(mesh):
    return jax.shard_map(
        functools.partial(shards, mesh.shape["seq"], mesh.shape["section"]),
        mesh=mesh,
        in_specs=(
            P("section", "seq", None),
            P("section", "seq", None, None),
            P("section", "seq", None, None),
            P("section", None),
            P("section", "seq", None),
            P("section", "seq", None),
            P("section", "seq", None),
            P("section", None),
        ),
        out_specs=P("section", "seq", None),
        check_vma=False,
    )
```
